32 devices in a mesh: grp: 8 (over y, x, core), loc: 4 (over z).
Axes of the slice: x: 2, y: 2, z: 4, core: 2. Of those that a mesh axis runs over, the one named last changes fastest.
Arguments:
- tokens: bfloat16 [4096, 7168], P(('grp', 'loc')), may hold values from -6 to 6
- route: int32 [4096, 1], P(('grp', 'loc')), may hold values from 0 to 7; in each aligned block of 128 rows (0 to 127, 128 to 255, ...) at most 20 rows name the same one
- gate_prob: float32 [4096, 1], P(('grp', 'loc')), may hold values from 0.25 to 1
- w_gate: bfloat16 [32, 7168, 256], P(('grp', 'loc')), may hold values from -0.0625 to 0.0625
- w_up: bfloat16 [32, 7168, 256], P(('grp', 'loc')), may hold values from -0.0625 to 0.0625
- w_down: bfloat16 [32, 256, 7168], P(('grp', 'loc')), may hold values from -0.1875 to 0.1875
- partner: int32 [32, 2], replicated, may hold values from 0 to 31, as said below
Outputs:
- mixed: bfloat16 [4096, 7168], P(('grp', 'loc'))
The draws below stay inside these ranges and needn't reach their ends.
Inputs may be any that keep to these rules, and one draw needn't show every extreme that they name: `route`: within the 128 rows of one device no expert is named more than 20 times, a bound that some block reaches. partner[i, h] is slot i itself, slot i - 1 or slot i + 1, cyclically over all slots.
All inputs are finite; a program needn't handle non-finite values.
Results may differ from the reference program's by a relative error of at most 0.0056.
Values may be sent and summed in bfloat16 or wider, within the bound.
A program may use at most 192 MiB of HBM per device.

```python
import math
import jax
import jax.numpy as jnp
import numpy as np
from jax import lax

D = 7168
FFW = 1024
SPAN = 4
TOP = 1
TOK_DEV = 128
HID = 256
EXPERTS = 8
TOKENS = 4096
CAP = 20
N_GRP = 8
N_LOC = 4


def draw_partner(key, part):
    slots_all = EXPERTS * SPAN
    index_all = jnp.arange(slots_all, dtype=jnp.int32)
    offsets = jax.random.randint(jax.random.fold_in(key, 11), (slots_all, 2), -1, 2).astype(jnp.int32)
    middle = slots_all // 2
    offsets = offsets.at[0, 0].set(-1).at[0, 1].set(1)
    offsets = offsets.at[middle, 0].set(-1).at[middle, 1].set(1)
    offsets = offsets.at[middle - 1, 0].set(1).at[middle - 1, 1].set(-1)
    offsets = offsets.at[slots_all - 1, 0].set(1).at[slots_all - 1, 1].set(-1)
    return ((index_all[:, None] + offsets) % slots_all).astype(jnp.int32)


def level_of(own_key, shape, pieces, least, largest):
    level = 1.0
    for dim, parts in pieces:
        steps = jax.random.uniform(jax.random.fold_in(jax.random.fold_in(own_key, 6), dim), (parts,), jnp.float32, least / len(pieces), largest / len(pieces))
        level = level * jnp.repeat(jnp.exp(steps), shape[dim] // parts).reshape((-1,) + (1,) * (len(shape) - 1 - dim))
    return level


def deal_out(own_key, own, number, rows, number_of, top, limit, skew):
    order = jax.random.permutation(own_key, number_of)
    packed, usual = portions_of(number_of, rows * top, limit, skew, True), portions_of(number_of, rows * top, limit, skew, False)
    places = jnp.arange(number_of)

    def named(tallies, turn):
        used = int((tallies > 0).sum())
        fixed = max(1, used // 4)
        passed = fixed + (places - fixed + turn * (used - fixed)) % max(1, number_of - fixed)
        return jnp.zeros((number_of,), jnp.int32).at[order[jnp.where(places < fixed, places, passed)]].set(jnp.asarray(tallies, jnp.int32))

    tallies = jnp.where(number % 4 == 0, named(packed, number // 4), named(usual, number - number // 4 - 1))
    mixed = jax.random.permutation(jax.random.fold_in(own, 3), number_of)
    source_of, sink = mixed[0:number_of // 2 * 2:2], mixed[1:number_of // 2 * 2:2]
    slack = jnp.minimum(tallies[source_of] - 1, limit - tallies[sink]) // 2
    slack = jnp.where((source_of == order[0]) | (sink == order[0]) | (tallies[sink] == 0), 0, jnp.maximum(slack, 0))
    passed = jax.random.randint(jax.random.fold_in(own, 4), (number_of // 2,), 0, 1 << 20) % (slack + 1)
    tallies = tallies.at[source_of].add(-passed).at[sink].add(passed)
    members = jnp.searchsorted(jnp.cumsum(tallies), jnp.arange(rows * top), side="right").astype(jnp.int32)
    grid = members.reshape(top, rows).T
    grid = grid[jax.random.permutation(jax.random.fold_in(own, 1), rows)]
    turn = jax.random.randint(jax.random.fold_in(own, 2), (rows, 1), 0, top)
    return jnp.take_along_axis(grid, (jnp.arange(top)[None, :] + turn) % top, axis=1)


def portions_of(amount, total, bound, skew, full):
    weights = [(1 << 20) // math.isqrt(grade ** skew) + 1 for grade in range(1, amount + 1)]
    largest = bound if full else min(bound, max(-(-total // amount), total * weights[0] // sum(weights)))
    least = 1 if total - largest >= amount - 1 else 0
    holding, spare = [largest] + [least] * (amount - 1), total - largest - least * (amount - 1)
    while spare > 0:
        candidates = [i for i in range(1, amount) if holding[i] < largest] or [i for i in range(1, amount) if holding[i] < bound]
        whole, remaining = sum([weights[i] for i in candidates]), spare
        for i in candidates:
            extra = min(bound - holding[i], max(1, remaining * weights[i] // whole), spare)
            holding[i] = holding[i] + extra
            spare = spare - extra
    return np.array(holding)


def bell_draw(rng, extent, spread, reach, cuts=(), kind=jnp.bfloat16):
    loudness = level_of(rng, extent, cuts, -0.22, 0.18) if cuts else 1.0
    array = jax.random.normal(rng, extent, jnp.float32) * spread * loudness
    return jnp.minimum(jnp.maximum(array, -reach), reach).astype(kind)


def setup_inputs(seed: int = 0) -> dict:
    seeds = jax.random.split(jax.random.key(seed), 8)
    tokens = bell_draw(seeds[0], (TOKENS, D), 1.0, 6.0, ((0, 32),))
    route_keys = jax.random.split(jax.random.fold_in(seeds[1], 1), TOKENS // TOK_DEV)
    route_turns = jax.random.permutation(jax.random.fold_in(seeds[1], 3), TOKENS // TOK_DEV)
    route = jax.vmap(lambda own, number: deal_out(jax.random.fold_in(seeds[1], 2), own, number, TOK_DEV, EXPERTS, TOP, CAP, 1))(route_keys, route_turns).reshape((TOKENS, TOP))
    gate_prob = jnp.clip(jnp.exp(math.log(1.0) - 1.3862944 * jax.random.uniform(seeds[2], (TOKENS, TOP), jnp.float32) ** level_of(seeds[2], (TOKENS, TOP), ((0, 32),), -0.2, 0.2)), 0.25, 1.0)
    w_gate = bell_draw(seeds[3], (N_GRP * N_LOC, D, HID), D ** -0.5, 0.0625, ((0, 32),))
    w_up = bell_draw(seeds[4], (N_GRP * N_LOC, D, HID), D ** -0.5, 0.0625, ((0, 32),))
    w_down = bell_draw(seeds[5], (N_GRP * N_LOC, HID, D), FFW ** -0.5, 0.1875, ((0, 32),))
    partner = draw_partner(jax.random.fold_in(seeds[7], 71), 0)
    return {"tokens": tokens, "route": route, "gate_prob": gate_prob, "w_gate": w_gate, "w_up": w_up, "w_down": w_down, "partner": partner}


def expert_pass(row_block, gate_block, up_block, down_block):
    gate_part = jnp.dot(row_block, gate_block, preferred_element_type=jnp.float32)
    up_part = jnp.dot(row_block, up_block, preferred_element_type=jnp.float32)
    hidden = (jax.nn.silu(gate_part) * up_part).astype(jnp.bfloat16)
    return jnp.dot(hidden, down_block, preferred_element_type=jnp.float32).astype(jnp.bfloat16)


def reference(tokens, route, gate_prob, w_gate, w_up, w_down, partner):
    slots_all = N_GRP * N_LOC
    per_source = TOK_DEV * TOP
    half = HID // 2
    routes = route.reshape(slots_all, per_source).astype(jnp.int32)
    onehot = (routes[:, :, None] == jnp.arange(EXPERTS, dtype=jnp.int32)[None, None, :]).astype(jnp.int32)
    slot_rank = (jnp.sum(jnp.cumsum(onehot, axis=1) * onehot, axis=2) - 1).astype(jnp.int32)
    assign_index = jnp.arange(slots_all * per_source, dtype=jnp.int32).reshape(slots_all, per_source)
    sources = jnp.broadcast_to(jnp.arange(slots_all, dtype=jnp.int32)[:, None], (slots_all, per_source))
    table = jnp.full((EXPERTS, slots_all, CAP), slots_all * per_source, jnp.int32)
    table = table.at[routes, sources, slot_rank].set(assign_index)
    padded = jnp.concatenate([jnp.repeat(tokens, TOP, axis=0), jnp.zeros((1, D), tokens.dtype)], axis=0)

    def expert_step(carry, expert_id):
        picks = table[expert_id].reshape(-1)
        row_block = padded[picks]
        total = jnp.zeros((slots_all * CAP, D), jnp.float32)
        for block_id in range(SPAN):
            first = partner[expert_id * SPAN + block_id, 0]
            second = partner[expert_id * SPAN + block_id, 1]
            gate_block = jnp.concatenate([w_gate[first][:, :half], w_gate[second][:, half:]], axis=1)
            up_block = jnp.concatenate([w_up[first][:, :half], w_up[second][:, half:]], axis=1)
            down_block = jnp.concatenate([w_down[first][:half], w_down[second][half:]], axis=0)
            total = total + expert_pass(row_block, gate_block, up_block, down_block).astype(jnp.float32)
        carry = carry.at[picks].set(total, mode="drop")
        return carry, expert_id

    mixed_rows = lax.scan(expert_step, jnp.zeros((slots_all * per_source, D), jnp.float32),
                          jnp.arange(EXPERTS, dtype=jnp.int32))[0]
    weighted = mixed_rows * gate_prob.reshape(-1)[:, None]
    return jnp.sum(weighted.reshape(TOKENS, TOP, D), axis=1).astype(jnp.bfloat16)
```

```python
import jax
import jax.numpy as jnp
from jax import lax
from jax.sharding import PartitionSpec as P

SPAN = 4
AXES = ("grp", "loc")


def half_pass(rows, w_gate, w_up, w_down, scale):
    gate_part = jnp.dot(rows, w_gate, preferred_element_type=jnp.float32)
    up_part = jnp.dot(rows, w_up, preferred_element_type=jnp.float32)
    hidden = (jax.nn.silu(gate_part) * up_part * scale[None, :]).astype(jnp.bfloat16)
    return jnp.dot(hidden, w_down, preferred_element_type=jnp.float32)


def body(tokens, route, gate_prob, w_gate, w_up, w_down, partner):
    slots_all = lax.axis_size(AXES)
    own = lax.axis_index(AXES)
    tok_count, top_count = route.shape
    width = tokens.shape[1]
    hid = w_gate.shape[2]
    capacity = max(2, tok_count * top_count * SPAN * 5 // (4 * slots_all))
    experts_all = slots_all // SPAN
    flat_route = route.reshape(-1)
    flat_gate = gate_prob.reshape(-1)
    own_expert = own // SPAN
    place = own % SPAN

    pairs = []
    for i in range(slots_all):
        if i % SPAN == 0:
            pairs.append((i, (i - SPAN) % slots_all))
        elif i % SPAN == SPAN - 1:
            pairs.append((i, (i + SPAN) % slots_all))
    edge_gate, edge_up, edge_down = [
        lax.ppermute(w[0], AXES, pairs) for w in (w_gate, w_up, w_down)
    ]
    mine = lax.dynamic_slice_in_dim(partner, own_expert * SPAN, SPAN, axis=0)
    edge_slot = jnp.where(place == 0, own + SPAN, own - SPAN + slots_all) % slots_all
    is_edge = (place == 0) | (place == SPAN - 1)
    own_times = jnp.sum(mine == own, axis=0).astype(jnp.float32)
    edge_times = jnp.sum((mine == edge_slot) & is_edge, axis=0).astype(jnp.float32)
    own_scale = jnp.repeat(own_times, hid // 2)
    edge_scale = jnp.repeat(edge_times, hid // 2)

    onehot = (flat_route[:, None] == jnp.arange(experts_all, dtype=jnp.int32)[None, :]).astype(
        jnp.int32
    )
    slot_rank = jnp.sum(jnp.cumsum(onehot, axis=0) * onehot, axis=1) - 1
    assigned = jnp.repeat(tokens, top_count, axis=0)
    position = flat_route * capacity + slot_rank
    rows = experts_all * capacity
    picker = (jnp.arange(rows, dtype=jnp.int32)[:, None] == position[None, :]).astype(jnp.bfloat16)
    outgoing = jnp.dot(picker, assigned, preferred_element_type=jnp.float32).astype(jnp.bfloat16)

    groups = [[e * SPAN + q for e in range(experts_all)] for q in range(SPAN)]
    spans = [[e * SPAN + q for q in range(SPAN)] for e in range(experts_all)]

    def across(block):
        if lax.axis_size("loc") == SPAN:
            return lax.all_to_all(block, "grp", split_axis=0, concat_axis=0, tiled=True)
        return lax.all_to_all(
            block, AXES, split_axis=0, concat_axis=0, tiled=True, axis_index_groups=groups
        )

    def within(block):
        if lax.axis_size("loc") == SPAN:
            return lax.all_to_all(block, "loc", split_axis=0, concat_axis=0, tiled=True)
        return lax.all_to_all(
            block, AXES, split_axis=0, concat_axis=0, tiled=True, axis_index_groups=spans
        )

    received = across(outgoing)
    if lax.axis_size("loc") == SPAN:
        gathered = lax.all_gather(received, "loc", axis=0, tiled=True)
    else:
        gathered = lax.all_gather(received, AXES, axis=0, tiled=True, axis_index_groups=spans)
    result = half_pass(gathered, w_gate[0], w_up[0], w_down[0], own_scale)
    result = result + half_pass(gathered, edge_gate, edge_up, edge_down, edge_scale)
    partial = result.astype(jnp.bfloat16)
    parts = within(partial).reshape(SPAN, rows, width)
    total = jnp.sum(parts.astype(jnp.float32), axis=0).astype(jnp.bfloat16)
    returned = across(total)
    expert_out = lax.dot_general(
        picker, returned, (((0,), (0,)), ((), ())), preferred_element_type=jnp.float32
    )
    weighted = expert_out * flat_gate[:, None]
    return jnp.sum(weighted.reshape(tok_count, top_count, width), axis=1).astype(jnp.bfloat16)


def solution(mesh):
    return jax.shard_map(
        body,
        mesh=mesh,
        in_specs=(
            P(AXES, None),
            P(AXES, None),
            P(AXES, None),
            P(AXES, None, None),
            P(AXES, None, None),
            P(AXES, None, None),
            P(),
        ),
        out_specs=P(AXES, None),
        check_vma=False,
    )
```

```python
import functools

import jax
import jax.numpy as jnp
from jax import lax
from jax.experimental import pallas as pl
from jax.experimental.pallas import tpu as pltpu
from jax.sharding import PartitionSpec as P

SPAN = 4
AXES = ("grp", "loc")


MESH = pl.DeviceIdType.MESH


def expert_kernel(
    slots_all,
    n_loc,
    chunks,
    x_ref,
    wg_hbm,
    wu_hbm,
    wd_hbm,
    scale_ref,
    o_ref,
    wg,
    wu,
    wd,
    eg,
    eu,
    ed,
    rows_buf,
    up_buf,
    down_buf,
    hid_buf,
    acc_buf,
    load_sem,
    edge_send,
    edge_recv,
    ag_send,
    ag_recv,
    rs_send,
    rs_recv,
    own_sem,
    out_sem,
):
    last = SPAN - 1
    own = lax.axis_index("grp") * n_loc + lax.axis_index("loc")
    place = lax.rem(own, SPAN)
    span_rows, width = rows_buf.shape[2], rows_buf.shape[3]
    hid = wg.shape[1]
    is_edge = (place == 0) | (place == last)

    def device(index):
        index = lax.rem(index + slots_all, slots_all)
        return (lax.div(index, n_loc), lax.rem(index, n_loc))

    barrier = pltpu.get_barrier_semaphore()

    def greet(index):
        pl.semaphore_signal(barrier, inc=1, device_id=device(index), device_id_type=MESH)

    pl.when(place < last)(lambda: greet(own + 1))
    pl.when(place > 0)(lambda: greet(own - 1))

    @pl.when(is_edge)
    def _():
        greet(own + SPAN)
        greet(own - SPAN)

    pl.semaphore_wait(barrier, jnp.where(is_edge, 3, 2))

    edge_target = device(jnp.where(place == 0, own - SPAN, own + SPAN))
    edge_copies = [
        pltpu.make_async_remote_copy(
            src_ref=src,
            dst_ref=dst,
            send_sem=edge_send.at[k],
            recv_sem=edge_recv.at[k],
            device_id=edge_target,
            device_id_type=MESH,
        )
        for k, (src, dst) in enumerate(((wg_hbm, eg), (wu_hbm, eu), (wd_hbm, ed)))
    ]
    loads = [
        pltpu.make_async_copy(src, dst, load_sem.at[k])
        for k, (src, dst) in enumerate(((wg_hbm, wg), (wu_hbm, wu), (wd_hbm, wd)))
    ]

    def mirrored(way, value):
        return value if way == 0 else last - value

    def gather_copy(way, c, step):
        mine = mirrored(way, place)
        source = mirrored(way, jnp.clip(mine - (step - 1), 0, last))
        return pltpu.make_async_remote_copy(
            src_ref=x_ref.at[c] if step == 1 else rows_buf.at[c, source],
            dst_ref=rows_buf.at[c, source],
            send_sem=ag_send.at[way, c, step - 1],
            recv_sem=ag_recv.at[way, c, step - 1],
            device_id=device(own + 1 if way == 0 else own - 1),
            device_id_type=MESH,
        )

    def gather_sends(way, step):
        mine = mirrored(way, place)
        return (mine < last) & (mine >= step - 1)

    def gather_gets(way, step):
        return mirrored(way, place) >= step

    def gather_start(c, step):
        for way in range(2):
            pl.when(gather_sends(way, step))(lambda way=way: gather_copy(way, c, step).start())

    def gather_wait(c, step):
        for way in range(2):
            pl.when(gather_gets(way, step))(lambda way=way: gather_copy(way, c, step).wait_recv())

    def gather_drain(c):
        for step in range(1, SPAN):
            for way in range(2):
                pl.when(gather_sends(way, step))(
                    lambda way=way, step=step: gather_copy(way, c, step).wait_send()
                )

    side = (up_buf, down_buf)

    def reduce_target(way, step):
        mine = mirrored(way, place)
        return mirrored(way, jnp.clip(SPAN + mine - step, 0, last))

    def reduce_copy(way, c, step, first):
        target = reduce_target(way, step)
        return pltpu.make_async_remote_copy(
            src_ref=rows_buf.at[c, target] if first else side[way].at[c, target],
            dst_ref=side[way].at[c, target],
            send_sem=rs_send.at[way, c, step - 1],
            recv_sem=rs_recv.at[way, c, step - 1],
            device_id=device(own + 1 if way == 0 else own - 1),
            device_id_type=MESH,
        )

    def reduce_sends(way, step):
        mine = mirrored(way, place)
        return (mine <= step - 1) & (mine < last) & (mine > 0)

    def reduce_gets(way, step):
        mine = mirrored(way, place)
        return (mine >= 1) & (mine <= step)

    cols = 512 if width % 512 == 0 else 128

    def reduce_start(c, step):
        for way in range(2):
            pl.when(mirrored(way, place) == 0)(
                lambda way=way: reduce_copy(way, c, step, True).start()
            )

            @pl.when(reduce_sends(way, step))
            def _(way=way):
                target = reduce_target(way, step)

                @pl.loop(0, width // cols)
                def _(k):
                    at = pl.ds(pl.multiple_of(k * cols, cols), cols)
                    side[way][c, target, :, at] = (
                        side[way][c, target, :, at].astype(jnp.float32)
                        + rows_buf[c, target, :, at].astype(jnp.float32)
                    ).astype(jnp.bfloat16)

                reduce_copy(way, c, step, False).start()

    def reduce_wait(c, step):
        for way in range(2):
            pl.when(reduce_gets(way, step))(
                lambda way=way: reduce_copy(way, c, step, False).wait_recv()
            )

    def reduce_drain(c):
        for step in range(1, SPAN):
            for way in range(2):
                mine = mirrored(way, place)
                pl.when((mine <= step - 1) & (mine < last))(
                    lambda way=way, step=step: reduce_copy(way, c, step, False).wait_send()
                )

    def out_copy(c):
        return pltpu.make_async_copy(rows_buf.at[c, place], o_ref.at[c], out_sem.at[c])

    def reduce_finish(c):
        @pl.loop(0, width // cols)
        def _(k):
            at = pl.ds(pl.multiple_of(k * cols, cols), cols)
            acc_buf[...] = rows_buf[c, place, :, at].astype(jnp.float32)
            for way in range(2):

                @pl.when(mirrored(way, place) > 0)
                def _(way=way):
                    acc_buf[...] += side[way][c, place, :, at].astype(jnp.float32)

            rows_buf[c, place, :, at] = acc_buf[...].astype(jnp.bfloat16)

        out_copy(c).start()

    total_rows = SPAN * span_rows
    depth = 512 if width % 512 == 0 else 128

    def make_hidden(c, gate_w, up_w, which):
        def step(k, carry):
            gate_part, up_part = carry
            at = pl.ds(pl.multiple_of(k * depth, depth), depth)
            block = rows_buf[c, :, :, at].reshape(total_rows, depth)
            gate_part += jnp.dot(block, gate_w[at, :], preferred_element_type=jnp.float32)
            up_part += jnp.dot(block, up_w[at, :], preferred_element_type=jnp.float32)
            return gate_part, up_part

        zero = jnp.zeros((total_rows, hid), jnp.float32)
        gate_part, up_part = lax.fori_loop(0, width // depth, step, (zero, zero))
        value = gate_part / (1.0 + jnp.exp(-gate_part)) * up_part
        hid_buf[which] = (value * scale_ref[which : which + 1, :]).astype(jnp.bfloat16)

    def make_partial(c, both):
        @pl.loop(0, width // cols)
        def _(k):
            at = pl.ds(pl.multiple_of(k * cols, cols), cols)
            out = jnp.dot(hid_buf[0], wd[:, at], preferred_element_type=jnp.float32)
            if both:
                out += jnp.dot(hid_buf[1], ed[:, at], preferred_element_type=jnp.float32)
            rows_buf[c, :, :, at] = out.astype(jnp.bfloat16).reshape(SPAN, span_rows, cols)

    def compute(c):
        if c == 0:
            for copy in loads:
                copy.wait()
        make_hidden(c, wg, wu, 0)

        @pl.when(is_edge)
        def _():
            if c == 0:
                for copy in edge_copies:
                    copy.wait_recv()
            make_hidden(c, eg, eu, 1)

        gather_drain(c)
        pl.when(is_edge)(lambda: make_partial(c, True))
        pl.when(jnp.logical_not(is_edge))(lambda: make_partial(c, False))

    own_copies = [
        pltpu.make_async_copy(x_ref.at[c], rows_buf.at[c, place], own_sem.at[c])
        for c in range(chunks)
    ]

    gather_start(0, 1)

    @pl.when(is_edge)
    def _():
        for copy in edge_copies:
            copy.start()

    for copy in own_copies + loads:
        copy.start()
    for step in range(1, SPAN):
        if step > 1:
            gather_start(0, step)
        gather_wait(0, step)
    for c in range(chunks):
        if c == 0:
            for copy in own_copies:
                copy.wait()
        if c + 1 < chunks:
            gather_start(c + 1, 1)
        if c > 0:
            pass
        compute(c)
        reduce_start(c, 1)
        if c + 1 < chunks:
            gather_wait(c + 1, 1)
            gather_start(c + 1, 2)
        reduce_wait(c, 1)
        reduce_start(c, 2)
        if c + 1 < chunks:
            gather_wait(c + 1, 2)
            gather_start(c + 1, 3)
        reduce_wait(c, 2)
        reduce_start(c, 3)
        if c + 1 < chunks:
            gather_wait(c + 1, 3)
        reduce_wait(c, 3)
        reduce_finish(c)
    for c in range(chunks):
        reduce_drain(c)
        out_copy(c).wait()

    @pl.when(is_edge)
    def _():
        for copy in edge_copies:
            copy.wait_send()


def run_experts(received, w_gate, w_up, w_down, scales, slots_all):
    rows, width = received.shape
    hid = w_gate.shape[1]
    chunks = 2 if rows % 32 == 0 else 1
    span_rows = rows // chunks
    anywhere = pl.BlockSpec(memory_space=pl.ANY)
    dma = pltpu.SemaphoreType.DMA
    bf16 = jnp.bfloat16
    out = pl.pallas_call(
        functools.partial(expert_kernel, slots_all, lax.axis_size("loc"), chunks),
        out_shape=jax.ShapeDtypeStruct((chunks, span_rows, width), bf16),
        in_specs=[anywhere] * 4 + [pl.BlockSpec(memory_space=pltpu.VMEM)],
        out_specs=anywhere,
        scratch_shapes=[
            pltpu.VMEM((width, hid), bf16),
            pltpu.VMEM((width, hid), bf16),
            pltpu.VMEM((hid, width), bf16),
            pltpu.VMEM((width, hid), bf16),
            pltpu.VMEM((width, hid), bf16),
            pltpu.VMEM((hid, width), bf16),
            pltpu.VMEM((chunks, SPAN, span_rows, width), bf16),
            pltpu.VMEM((chunks, SPAN, span_rows, width), bf16),
            pltpu.VMEM((chunks, SPAN, span_rows, width), bf16),
            pltpu.VMEM((2, SPAN * span_rows, hid), bf16),
            pltpu.VMEM((span_rows, 512 if width % 512 == 0 else 128), jnp.float32),
            dma((3,)),
            dma((3,)),
            dma((3,)),
            dma((2, chunks, SPAN - 1)),
            dma((2, chunks, SPAN - 1)),
            dma((2, chunks, SPAN - 1)),
            dma((2, chunks, SPAN - 1)),
            dma((chunks,)),
            dma((chunks,)),
        ],
        compiler_params=pltpu.CompilerParams(
            collective_id=0, has_side_effects=True, vmem_limit_bytes=62 * 1024 * 1024
        ),
        name="experts",
    )(received.reshape(chunks, span_rows, width), w_gate, w_up, w_down, scales)
    return out.reshape(rows, width)


def body(tokens, route, gate_prob, w_gate, w_up, w_down, partner):
    slots_all = lax.axis_size(AXES)
    own = lax.axis_index(AXES)
    tok_count, top_count = route.shape
    width = tokens.shape[1]
    hid = w_gate.shape[2]
    capacity = max(2, tok_count * top_count * SPAN * 5 // (4 * slots_all))
    experts_all = slots_all // SPAN
    flat_route = route.reshape(-1)
    flat_gate = gate_prob.reshape(-1)
    own_expert = own // SPAN
    place = own % SPAN

    mine = lax.dynamic_slice_in_dim(partner, own_expert * SPAN, SPAN, axis=0)
    edge_slot = jnp.where(place == 0, own + SPAN, own - SPAN + slots_all) % slots_all
    is_edge = (place == 0) | (place == SPAN - 1)
    own_times = jnp.sum(mine == own, axis=0).astype(jnp.float32)
    edge_times = jnp.sum((mine == edge_slot) & is_edge, axis=0).astype(jnp.float32)
    scales = jnp.repeat(jnp.stack([own_times, edge_times]), hid // 2, axis=1)

    onehot = (flat_route[:, None] == jnp.arange(experts_all, dtype=jnp.int32)[None, :]).astype(
        jnp.int32
    )
    slot_rank = jnp.sum(jnp.cumsum(onehot, axis=0) * onehot, axis=1) - 1
    assigned = jnp.repeat(tokens, top_count, axis=0)
    position = flat_route * capacity + slot_rank
    rows = experts_all * capacity
    picker = (jnp.arange(rows, dtype=jnp.int32)[:, None] == position[None, :]).astype(jnp.bfloat16)
    outgoing = jnp.dot(picker, assigned, preferred_element_type=jnp.float32).astype(jnp.bfloat16)

    groups = [[e * SPAN + q for e in range(experts_all)] for q in range(SPAN)]
    def across(block):
        if lax.axis_size("loc") == SPAN:
            return lax.all_to_all(block, "grp", split_axis=0, concat_axis=0, tiled=True)
        return lax.all_to_all(
            block, AXES, split_axis=0, concat_axis=0, tiled=True, axis_index_groups=groups
        )

    received = across(outgoing)
    total = run_experts(
        received.reshape(rows, width), w_gate[0], w_up[0], w_down[0], scales, slots_all
    )
    returned = across(total)
    expert_out = lax.dot_general(
        picker, returned, (((0,), (0,)), ((), ())), preferred_element_type=jnp.float32
    )
    weighted = expert_out * flat_gate[:, None]
    return jnp.sum(weighted.reshape(tok_count, top_count, width), axis=1).astype(jnp.bfloat16)


def solution(mesh):
    return jax.shard_map(
        body,
        mesh=mesh,
        in_specs=(
            P(AXES, None),
            P(AXES, None),
            P(AXES, None),
            P(AXES, None, None),
            P(AXES, None, None),
            P(AXES, None, None),
            P(),
        ),
        out_specs=P(AXES, None),
        check_vma=False,
    )
```

```python
import functools

import jax
import jax.numpy as jnp
from jax import lax
from jax.experimental import pallas as pl
from jax.experimental.pallas import tpu as pltpu
from jax.sharding import PartitionSpec as P

SPAN = 4
AXES = ("grp", "loc")


MESH = pl.DeviceIdType.MESH


def expert_kernel(
    slots_all,
    n_loc,
    chunks,
    x_ref,
    wg_hbm,
    wu_hbm,
    wd_hbm,
    scale_ref,
    o_ref,
    wg,
    wu,
    wd,
    eg,
    eu,
    ed,
    rows_buf,
    up_buf,
    down_buf,
    hid_buf,
    acc_buf,
    load_sem,
    edge_send,
    edge_recv,
    ag_send,
    ag_recv,
    rs_send,
    rs_recv,
    own_sem,
    out_sem,
):
    last = SPAN - 1
    own = lax.axis_index("grp") * n_loc + lax.axis_index("loc")
    place = lax.rem(own, SPAN)
    span_rows, width = rows_buf.shape[2], rows_buf.shape[3]
    hid = wg.shape[1]
    is_edge = (place == 0) | (place == last)

    def device(index):
        index = lax.rem(index + slots_all, slots_all)
        return (lax.div(index, n_loc), lax.rem(index, n_loc))

    barrier = pltpu.get_barrier_semaphore()

    def greet(index):
        pl.semaphore_signal(barrier, inc=1, device_id=device(index), device_id_type=MESH)

    pl.when(place < last)(lambda: greet(own + 1))
    pl.when(place > 0)(lambda: greet(own - 1))

    @pl.when(is_edge)
    def _():
        greet(own + SPAN)
        greet(own - SPAN)

    pl.semaphore_wait(barrier, jnp.where(is_edge, 3, 2))

    edge_target = device(jnp.where(place == 0, own - SPAN, own + SPAN))
    edge_copies = [
        pltpu.make_async_remote_copy(
            src_ref=src,
            dst_ref=dst,
            send_sem=edge_send.at[k],
            recv_sem=edge_recv.at[k],
            device_id=edge_target,
            device_id_type=MESH,
        )
        for k, (src, dst) in enumerate(((wg_hbm, eg), (wu_hbm, eu), (wd_hbm, ed)))
    ]
    loads = [
        pltpu.make_async_copy(src, dst, load_sem.at[k])
        for k, (src, dst) in enumerate(((wg_hbm, wg), (wu_hbm, wu), (wd_hbm, wd)))
    ]

    def mirrored(way, value):
        return value if way == 0 else last - value

    def gather_copy(way, c, step):
        mine = mirrored(way, place)
        source = mirrored(way, jnp.clip(mine - (step - 1), 0, last))
        return pltpu.make_async_remote_copy(
            src_ref=x_ref.at[c] if step == 1 else rows_buf.at[c, source],
            dst_ref=rows_buf.at[c, source],
            send_sem=ag_send.at[way, c, step - 1],
            recv_sem=ag_recv.at[way, c, step - 1],
            device_id=device(own + 1 if way == 0 else own - 1),
            device_id_type=MESH,
        )

    def gather_sends(way, step):
        mine = mirrored(way, place)
        return (mine < last) & (mine >= step - 1)

    def gather_gets(way, step):
        return mirrored(way, place) >= step

    def gather_start(c, step):
        for way in range(2):
            pl.when(gather_sends(way, step))(lambda way=way: gather_copy(way, c, step).start())

    def gather_wait(c, step):
        for way in range(2):
            pl.when(gather_gets(way, step))(lambda way=way: gather_copy(way, c, step).wait_recv())

    def gather_drain(c):
        for step in range(1, SPAN):
            for way in range(2):
                pl.when(gather_sends(way, step))(
                    lambda way=way, step=step: gather_copy(way, c, step).wait_send()
                )

    side = (up_buf, down_buf)

    def reduce_target(way, step):
        mine = mirrored(way, place)
        return mirrored(way, jnp.clip(SPAN + mine - step, 0, last))

    def reduce_copy(way, c, step, first):
        target = reduce_target(way, step)
        return pltpu.make_async_remote_copy(
            src_ref=rows_buf.at[c, target] if first else side[way].at[c, target],
            dst_ref=side[way].at[c, target],
            send_sem=rs_send.at[way, c, step - 1],
            recv_sem=rs_recv.at[way, c, step - 1],
            device_id=device(own + 1 if way == 0 else own - 1),
            device_id_type=MESH,
        )

    def reduce_sends(way, step):
        mine = mirrored(way, place)
        return (mine <= step - 1) & (mine < last) & (mine > 0)

    def reduce_gets(way, step):
        mine = mirrored(way, place)
        return (mine >= 1) & (mine <= step)

    cols = 512 if width % 512 == 0 else 128

    def reduce_start(c, step):
        for way in range(2):
            pl.when(mirrored(way, place) == 0)(
                lambda way=way: reduce_copy(way, c, step, True).start()
            )

            @pl.when(reduce_sends(way, step))
            def _(way=way):
                target = reduce_target(way, step)

                @pl.loop(0, width // cols)
                def _(k):
                    at = pl.ds(pl.multiple_of(k * cols, cols), cols)
                    side[way][c, target, :, at] = (
                        side[way][c, target, :, at].astype(jnp.float32)
                        + rows_buf[c, target, :, at].astype(jnp.float32)
                    ).astype(jnp.bfloat16)

                reduce_copy(way, c, step, False).start()

    def reduce_wait(c, step):
        for way in range(2):
            pl.when(reduce_gets(way, step))(
                lambda way=way: reduce_copy(way, c, step, False).wait_recv()
            )

    def reduce_drain(c):
        for step in range(1, SPAN):
            for way in range(2):
                mine = mirrored(way, place)
                pl.when((mine <= step - 1) & (mine < last))(
                    lambda way=way, step=step: reduce_copy(way, c, step, False).wait_send()
                )

    def out_copy(c):
        return pltpu.make_async_copy(rows_buf.at[c, place], o_ref.at[c], out_sem.at[c])

    def reduce_finish(c):
        @pl.loop(0, width // cols)
        def _(k):
            at = pl.ds(pl.multiple_of(k * cols, cols), cols)
            acc_buf[...] = rows_buf[c, place, :, at].astype(jnp.float32)
            for way in range(2):

                @pl.when(mirrored(way, place) > 0)
                def _(way=way):
                    acc_buf[...] += side[way][c, place, :, at].astype(jnp.float32)

            rows_buf[c, place, :, at] = acc_buf[...].astype(jnp.bfloat16)

        out_copy(c).start()

    total_rows = SPAN * span_rows
    depth = 512 if width % 512 == 0 else 128

    def make_hidden(c, gate_w, up_w, which):
        def step(k, carry):
            gate_part, up_part = carry
            at = pl.ds(pl.multiple_of(k * depth, depth), depth)
            block = rows_buf[c, :, :, at].reshape(total_rows, depth)
            gate_part += jnp.dot(block, gate_w[at, :], preferred_element_type=jnp.float32)
            up_part += jnp.dot(block, up_w[at, :], preferred_element_type=jnp.float32)
            return gate_part, up_part

        zero = jnp.zeros((total_rows, hid), jnp.float32)
        gate_part, up_part = lax.fori_loop(0, width // depth, step, (zero, zero))
        value = gate_part / (1.0 + jnp.exp(-gate_part)) * up_part
        hid_buf[which] = (value * scale_ref[which : which + 1, :]).astype(jnp.bfloat16)

    def make_partial(c, both):
        @pl.loop(0, width // cols)
        def _(k):
            at = pl.ds(pl.multiple_of(k * cols, cols), cols)
            out = jnp.dot(hid_buf[0], wd[:, at], preferred_element_type=jnp.float32)
            if both:
                out += jnp.dot(hid_buf[1], ed[:, at], preferred_element_type=jnp.float32)
            rows_buf[c, :, :, at] = out.astype(jnp.bfloat16).reshape(SPAN, span_rows, cols)

    def compute(c):
        if c == 0:
            for copy in loads:
                copy.wait()
        make_hidden(c, wg, wu, 0)

        @pl.when(is_edge)
        def _():
            if c == 0:
                for copy in edge_copies[:2]:
                    copy.wait_recv()
            make_hidden(c, eg, eu, 1)
            if c == 0:
                edge_copies[2].wait_recv()

        gather_drain(c)
        pl.when(is_edge)(lambda: make_partial(c, True))
        pl.when(jnp.logical_not(is_edge))(lambda: make_partial(c, False))

    own_copies = [
        pltpu.make_async_copy(x_ref.at[c], rows_buf.at[c, place], own_sem.at[c])
        for c in range(chunks)
    ]

    gather_start(0, 1)

    @pl.when(is_edge)
    def _():
        for copy in edge_copies:
            copy.start()

    for copy in own_copies + loads:
        copy.start()
    for step in range(1, SPAN):
        if step > 1:
            gather_start(0, step)
        gather_wait(0, step)
    for copy in own_copies:
        copy.wait()
    if chunks > 1:
        gather_start(1, 1)
    compute(0)
    for c in range(chunks):
        more = c + 1 < chunks
        reduce_start(c, 1)
        if c > 0:
            reduce_finish(c - 1)
        for step in range(1, SPAN - 1):
            if more:
                gather_wait(c + 1, step)
                gather_start(c + 1, step + 1)
            reduce_wait(c, step)
            reduce_start(c, step + 1)
        if more:
            gather_wait(c + 1, SPAN - 1)
            if c + 2 < chunks:
                gather_start(c + 2, 1)
            compute(c + 1)
        reduce_wait(c, SPAN - 1)
    reduce_finish(chunks - 1)
    for c in range(chunks):
        reduce_drain(c)
        out_copy(c).wait()

    @pl.when(is_edge)
    def _():
        for copy in edge_copies:
            copy.wait_send()


def run_experts(received, w_gate, w_up, w_down, scales, slots_all):
    rows, width = received.shape
    hid = w_gate.shape[1]
    chunks = 2 if rows % 32 == 0 else 1
    span_rows = rows // chunks
    anywhere = pl.BlockSpec(memory_space=pl.ANY)
    dma = pltpu.SemaphoreType.DMA
    bf16 = jnp.bfloat16
    out = pl.pallas_call(
        functools.partial(expert_kernel, slots_all, lax.axis_size("loc"), chunks),
        out_shape=jax.ShapeDtypeStruct((chunks, span_rows, width), bf16),
        in_specs=[anywhere] * 4 + [pl.BlockSpec(memory_space=pltpu.VMEM)],
        out_specs=anywhere,
        scratch_shapes=[
            pltpu.VMEM((width, hid), bf16),
            pltpu.VMEM((width, hid), bf16),
            pltpu.VMEM((hid, width), bf16),
            pltpu.VMEM((width, hid), bf16),
            pltpu.VMEM((width, hid), bf16),
            pltpu.VMEM((hid, width), bf16),
            pltpu.VMEM((chunks, SPAN, span_rows, width), bf16),
            pltpu.VMEM((chunks, SPAN, span_rows, width), bf16),
            pltpu.VMEM((chunks, SPAN, span_rows, width), bf16),
            pltpu.VMEM((2, SPAN * span_rows, hid), bf16),
            pltpu.VMEM((span_rows, 512 if width % 512 == 0 else 128), jnp.float32),
            dma((3,)),
            dma((3,)),
            dma((3,)),
            dma((2, chunks, SPAN - 1)),
            dma((2, chunks, SPAN - 1)),
            dma((2, chunks, SPAN - 1)),
            dma((2, chunks, SPAN - 1)),
            dma((chunks,)),
            dma((chunks,)),
        ],
        compiler_params=pltpu.CompilerParams(
            collective_id=0, has_side_effects=True, vmem_limit_bytes=62 * 1024 * 1024
        ),
        name="experts",
    )(received.reshape(chunks, span_rows, width), w_gate, w_up, w_down, scales)
    return out.reshape(rows, width)


def body(tokens, route, gate_prob, w_gate, w_up, w_down, partner):
    slots_all = lax.axis_size(AXES)
    own = lax.axis_index(AXES)
    tok_count, top_count = route.shape
    width = tokens.shape[1]
    hid = w_gate.shape[2]
    capacity = max(2, tok_count * top_count * SPAN * 5 // (4 * slots_all))
    experts_all = slots_all // SPAN
    flat_route = route.reshape(-1)
    flat_gate = gate_prob.reshape(-1)
    own_expert = own // SPAN
    place = own % SPAN

    mine = lax.dynamic_slice_in_dim(partner, own_expert * SPAN, SPAN, axis=0)
    edge_slot = jnp.where(place == 0, own + SPAN, own - SPAN + slots_all) % slots_all
    is_edge = (place == 0) | (place == SPAN - 1)
    own_times = jnp.sum(mine == own, axis=0).astype(jnp.float32)
    edge_times = jnp.sum((mine == edge_slot) & is_edge, axis=0).astype(jnp.float32)
    scales = jnp.repeat(jnp.stack([own_times, edge_times]), hid // 2, axis=1)

    onehot = (flat_route[:, None] == jnp.arange(experts_all, dtype=jnp.int32)[None, :]).astype(
        jnp.int32
    )
    slot_rank = jnp.sum(jnp.cumsum(onehot, axis=0) * onehot, axis=1) - 1
    assigned = jnp.repeat(tokens, top_count, axis=0)
    position = flat_route * capacity + slot_rank
    rows = experts_all * capacity
    picker = (jnp.arange(rows, dtype=jnp.int32)[:, None] == position[None, :]).astype(jnp.bfloat16)
    outgoing = jnp.dot(picker, assigned, preferred_element_type=jnp.float32).astype(jnp.bfloat16)

    groups = [[e * SPAN + q for e in range(experts_all)] for q in range(SPAN)]
    def across(block):
        if lax.axis_size("loc") == SPAN:
            return lax.all_to_all(block, "grp", split_axis=0, concat_axis=0, tiled=True)
        return lax.all_to_all(
            block, AXES, split_axis=0, concat_axis=0, tiled=True, axis_index_groups=groups
        )

    received = across(outgoing)
    total = run_experts(
        received.reshape(rows, width), w_gate[0], w_up[0], w_down[0], scales, slots_all
    )
    returned = across(total)
    expert_out = lax.dot_general(
        picker, returned, (((0,), (0,)), ((), ())), preferred_element_type=jnp.float32
    )
    weighted = expert_out * flat_gate[:, None]
    return jnp.sum(weighted.reshape(tok_count, top_count, width), axis=1).astype(jnp.bfloat16)


def solution(mesh):
    return jax.shard_map(
        body,
        mesh=mesh,
        in_specs=(
            P(AXES, None),
            P(AXES, None),
            P(AXES, None),
            P(AXES, None, None),
            P(AXES, None, None),
            P(AXES, None, None),
            P(),
        ),
        out_specs=P(AXES, None),
        check_vma=False,
    )
```

```python
import functools

import jax
import jax.numpy as jnp
from jax import lax
from jax.experimental import pallas as pl
from jax.experimental.pallas import tpu as pltpu
from jax.sharding import PartitionSpec as P

SPAN = 4
AXES = ("grp", "loc")


MESH = pl.DeviceIdType.MESH


def expert_kernel(
    slots_all,
    n_loc,
    chunks,
    x_ref,
    wg_hbm,
    wu_hbm,
    wd_hbm,
    scale_ref,
    o_ref,
    wg,
    wu,
    wd,
    eg,
    eu,
    ed,
    rows_buf,
    up_buf,
    down_buf,
    hid_buf,
    acc_buf,
    load_sem,
    edge_send,
    edge_recv,
    ag_send,
    ag_recv,
    rs_send,
    rs_recv,
    stage_in,
    stage_out,
    disp_send,
    disp_recv,
    ret_send,
    ret_recv,
    own_sem,
    out_sem,
):
    last = SPAN - 1
    own = lax.axis_index("grp") * n_loc + lax.axis_index("loc")
    place = lax.rem(own, SPAN)
    own_e = lax.div(own, SPAN)
    experts, capacity = x_ref.shape[0], x_ref.shape[1]
    per = experts // chunks
    span_rows, width = rows_buf.shape[2], rows_buf.shape[3]
    hid = wg.shape[1]
    is_edge = (place == 0) | (place == last)

    def device(index):
        index = lax.rem(index + slots_all, slots_all)
        return (lax.div(index, n_loc), lax.rem(index, n_loc))

    barrier = pltpu.get_barrier_semaphore()

    def greet(index):
        pl.semaphore_signal(barrier, inc=1, device_id=device(index), device_id_type=MESH)

    pl.when(place < last)(lambda: greet(own + 1))
    pl.when(place > 0)(lambda: greet(own - 1))

    @pl.when(is_edge)
    def _():
        greet(own + SPAN)
        greet(own - SPAN)

    for away in range(1, experts):
        greet(own + away * SPAN)
    pl.semaphore_wait(barrier, jnp.where(is_edge, 3, 2) + experts - 1)

    def dispatch_copy(away):
        peer = lax.rem(own_e + away, experts)
        return pltpu.make_async_remote_copy(
            src_ref=x_ref.at[peer],
            dst_ref=stage_in.at[own_e],
            send_sem=disp_send.at[away],
            recv_sem=disp_recv.at[away],
            device_id=device(peer * SPAN + place),
            device_id_type=MESH,
        )

    def return_copy(peer, sender):
        return pltpu.make_async_remote_copy(
            src_ref=stage_out.at[peer],
            dst_ref=o_ref.at[sender],
            send_sem=ret_send.at[peer],
            recv_sem=ret_recv.at[sender],
            device_id=device(peer * SPAN + place),
            device_id_type=MESH,
        )

    edge_target = device(jnp.where(place == 0, own - SPAN, own + SPAN))
    edge_copies = [
        pltpu.make_async_remote_copy(
            src_ref=src,
            dst_ref=dst,
            send_sem=edge_send.at[k],
            recv_sem=edge_recv.at[k],
            device_id=edge_target,
            device_id_type=MESH,
        )
        for k, (src, dst) in enumerate(((wg_hbm, eg), (wu_hbm, eu), (wd_hbm, ed)))
    ]
    loads = [
        pltpu.make_async_copy(src, dst, load_sem.at[k])
        for k, (src, dst) in enumerate(((wg_hbm, wg), (wu_hbm, wu), (wd_hbm, wd)))
    ]

    def mirrored(way, value):
        return value if way == 0 else last - value

    def gather_copy(way, c, step):
        mine = mirrored(way, place)
        source = mirrored(way, jnp.clip(mine - (step - 1), 0, last))
        return pltpu.make_async_remote_copy(
            src_ref=rows_buf.at[c, source],
            dst_ref=rows_buf.at[c, source],
            send_sem=ag_send.at[way, c, step - 1],
            recv_sem=ag_recv.at[way, c, step - 1],
            device_id=device(own + 1 if way == 0 else own - 1),
            device_id_type=MESH,
        )

    def gather_sends(way, step):
        mine = mirrored(way, place)
        return (mine < last) & (mine >= step - 1)

    def gather_gets(way, step):
        return mirrored(way, place) >= step

    def gather_start(c, step):
        for way in range(2):
            pl.when(gather_sends(way, step))(lambda way=way: gather_copy(way, c, step).start())

    def gather_wait(c, step):
        for way in range(2):
            pl.when(gather_gets(way, step))(lambda way=way: gather_copy(way, c, step).wait_recv())

    def gather_drain(c):
        for step in range(1, SPAN):
            for way in range(2):
                pl.when(gather_sends(way, step))(
                    lambda way=way, step=step: gather_copy(way, c, step).wait_send()
                )

    side = (up_buf, down_buf)

    def reduce_target(way, step):
        mine = mirrored(way, place)
        return mirrored(way, jnp.clip(SPAN + mine - step, 0, last))

    def reduce_copy(way, c, step, first):
        target = reduce_target(way, step)
        return pltpu.make_async_remote_copy(
            src_ref=rows_buf.at[c, target] if first else side[way].at[c, target],
            dst_ref=side[way].at[c, target],
            send_sem=rs_send.at[way, c, step - 1],
            recv_sem=rs_recv.at[way, c, step - 1],
            device_id=device(own + 1 if way == 0 else own - 1),
            device_id_type=MESH,
        )

    def reduce_sends(way, step):
        mine = mirrored(way, place)
        return (mine <= step - 1) & (mine < last) & (mine > 0)

    def reduce_gets(way, step):
        mine = mirrored(way, place)
        return (mine >= 1) & (mine <= step)

    cols = 512 if width % 512 == 0 else 128

    def reduce_start(c, step):
        for way in range(2):
            pl.when(mirrored(way, place) == 0)(
                lambda way=way: reduce_copy(way, c, step, True).start()
            )

            @pl.when(reduce_sends(way, step))
            def _(way=way):
                target = reduce_target(way, step)

                @pl.loop(0, width // cols)
                def _(k):
                    at = pl.ds(pl.multiple_of(k * cols, cols), cols)
                    side[way][c, target, :, at] = (
                        side[way][c, target, :, at].astype(jnp.float32)
                        + rows_buf[c, target, :, at].astype(jnp.float32)
                    ).astype(jnp.bfloat16)

                reduce_copy(way, c, step, False).start()

    def reduce_wait(c, step):
        for way in range(2):
            pl.when(reduce_gets(way, step))(
                lambda way=way: reduce_copy(way, c, step, False).wait_recv()
            )

    def reduce_drain(c):
        for step in range(1, SPAN):
            for way in range(2):
                mine = mirrored(way, place)
                pl.when((mine <= step - 1) & (mine < last))(
                    lambda way=way, step=step: reduce_copy(way, c, step, False).wait_send()
                )

    kept = pltpu.make_async_copy(stage_out.at[own_e], o_ref.at[own_e], out_sem)

    def unpack():
        @pl.loop(0, width // cols)
        def _(k):
            at = pl.ds(pl.multiple_of(k * cols, cols), cols)
            for j in range(experts):
                acc_buf[pl.ds(j * capacity, capacity), :] = stage_in[j, :, at].astype(jnp.float32)
            for c in range(chunks):
                rows_buf[c, place, :, at] = acc_buf[
                    pl.ds(c * span_rows, span_rows), :
                ].astype(jnp.bfloat16)

    def reduce_finish(c):
        first = pl.ds(0, span_rows)

        @pl.loop(0, width // cols)
        def _(k):
            at = pl.ds(pl.multiple_of(k * cols, cols), cols)
            acc_buf[first, :] = rows_buf[c, place, :, at].astype(jnp.float32)
            for way in range(2):

                @pl.when(mirrored(way, place) > 0)
                def _(way=way):
                    acc_buf[first, :] += side[way][c, place, :, at].astype(jnp.float32)

            for j in range(per):
                stage_out[c * per + j, :, at] = acc_buf[
                    pl.ds(j * capacity, capacity), :
                ].astype(jnp.bfloat16)

        for j in range(per):
            peer = c * per + j
            pl.when(own_e != peer)(lambda peer=peer: return_copy(peer, own_e).start())
            pl.when(own_e == peer)(lambda: kept.start())

    total_rows = SPAN * span_rows
    depth = 512 if width % 512 == 0 else 128

    def make_hidden(c, gate_w, up_w, which):
        def step(k, carry):
            gate_part, up_part = carry
            at = pl.ds(pl.multiple_of(k * depth, depth), depth)
            block = rows_buf[c, :, :, at].reshape(total_rows, depth)
            gate_part += jnp.dot(block, gate_w[at, :], preferred_element_type=jnp.float32)
            up_part += jnp.dot(block, up_w[at, :], preferred_element_type=jnp.float32)
            return gate_part, up_part

        zero = jnp.zeros((total_rows, hid), jnp.float32)
        gate_part, up_part = lax.fori_loop(0, width // depth, step, (zero, zero))
        value = gate_part / (1.0 + jnp.exp(-gate_part)) * up_part
        hid_buf[which] = (value * scale_ref[which : which + 1, :]).astype(jnp.bfloat16)

    def make_partial(c, both):
        @pl.loop(0, width // cols)
        def _(k):
            at = pl.ds(pl.multiple_of(k * cols, cols), cols)
            out = jnp.dot(hid_buf[0], wd[:, at], preferred_element_type=jnp.float32)
            if both:
                out += jnp.dot(hid_buf[1], ed[:, at], preferred_element_type=jnp.float32)
            rows_buf[c, :, :, at] = out.astype(jnp.bfloat16).reshape(SPAN, span_rows, cols)

    def compute(c):
        if c == 0:
            for copy in loads:
                copy.wait()
        make_hidden(c, wg, wu, 0)

        @pl.when(is_edge)
        def _():
            if c == 0:
                for copy in edge_copies[:2]:
                    copy.wait_recv()
            make_hidden(c, eg, eu, 1)
            if c == 0:
                edge_copies[2].wait_recv()

        gather_drain(c)
        pl.when(is_edge)(lambda: make_partial(c, True))
        pl.when(jnp.logical_not(is_edge))(lambda: make_partial(c, False))

    own_copy = pltpu.make_async_copy(x_ref.at[own_e], stage_in.at[own_e], own_sem)
    own_copy.start()
    for away in range(1, experts):
        dispatch_copy(away).start()

    @pl.when(is_edge)
    def _():
        for copy in edge_copies:
            copy.start()

    for copy in loads:
        copy.start()
    own_copy.wait()
    for away in range(1, experts):
        dispatch_copy(away).wait_recv()
    unpack()
    gather_start(0, 1)
    for step in range(1, SPAN):
        if step > 1:
            gather_start(0, step)
        gather_wait(0, step)
    if chunks > 1:
        gather_start(1, 1)
    compute(0)
    for c in range(chunks):
        more = c + 1 < chunks
        reduce_start(c, 1)
        if c > 0:
            reduce_finish(c - 1)
        for step in range(1, SPAN - 1):
            if more:
                gather_wait(c + 1, step)
                gather_start(c + 1, step + 1)
            reduce_wait(c, step)
            reduce_start(c, step + 1)
        if more:
            gather_wait(c + 1, SPAN - 1)
            if c + 2 < chunks:
                gather_start(c + 2, 1)
            compute(c + 1)
        reduce_wait(c, SPAN - 1)
    reduce_finish(chunks - 1)
    for c in range(chunks):
        reduce_drain(c)
    for away in range(1, experts):
        dispatch_copy(away).wait_send()
    for peer in range(experts):

        @pl.when(own_e != peer)
        def _(peer=peer):
            return_copy(peer, peer).wait_send()
            return_copy(peer, peer).wait_recv()

    kept.wait()

    @pl.when(is_edge)
    def _():
        for copy in edge_copies:
            copy.wait_send()


def run_experts(received, w_gate, w_up, w_down, scales, slots_all):
    experts, capacity, width = received.shape
    rows = experts * capacity
    hid = w_gate.shape[1]
    chunks = 2 if rows % 32 == 0 and experts % 2 == 0 else 1
    span_rows = rows // chunks
    anywhere = pl.BlockSpec(memory_space=pl.ANY)
    dma = pltpu.SemaphoreType.DMA
    bf16 = jnp.bfloat16
    out = pl.pallas_call(
        functools.partial(expert_kernel, slots_all, lax.axis_size("loc"), chunks),
        out_shape=jax.ShapeDtypeStruct((experts, capacity, width), bf16),
        in_specs=[anywhere] * 4 + [pl.BlockSpec(memory_space=pltpu.VMEM)],
        out_specs=anywhere,
        scratch_shapes=[
            pltpu.VMEM((width, hid), bf16),
            pltpu.VMEM((width, hid), bf16),
            pltpu.VMEM((hid, width), bf16),
            pltpu.VMEM((width, hid), bf16),
            pltpu.VMEM((width, hid), bf16),
            pltpu.VMEM((hid, width), bf16),
            pltpu.VMEM((chunks, SPAN, span_rows, width), bf16),
            pltpu.VMEM((chunks, SPAN, span_rows, width), bf16),
            pltpu.VMEM((chunks, SPAN, span_rows, width), bf16),
            pltpu.VMEM((2, SPAN * span_rows, hid), bf16),
            pltpu.VMEM((rows, 512 if width % 512 == 0 else 128), jnp.float32),
            dma((3,)),
            dma((3,)),
            dma((3,)),
            dma((2, chunks, SPAN - 1)),
            dma((2, chunks, SPAN - 1)),
            dma((2, chunks, SPAN - 1)),
            dma((2, chunks, SPAN - 1)),
            pltpu.VMEM((experts, capacity, width), bf16),
            pltpu.VMEM((experts, capacity, width), bf16),
            dma((experts,)),
            dma((experts,)),
            dma((experts,)),
            dma((experts,)),
            dma,
            dma,
        ],
        compiler_params=pltpu.CompilerParams(
            collective_id=0, has_side_effects=True, vmem_limit_bytes=62 * 1024 * 1024
        ),
        name="experts",
    )(received, w_gate, w_up, w_down, scales)
    return out


def body(tokens, route, gate_prob, w_gate, w_up, w_down, partner):
    slots_all = lax.axis_size(AXES)
    own = lax.axis_index(AXES)
    tok_count, top_count = route.shape
    width = tokens.shape[1]
    hid = w_gate.shape[2]
    capacity = max(2, tok_count * top_count * SPAN * 5 // (4 * slots_all))
    experts_all = slots_all // SPAN
    flat_route = route.reshape(-1)
    flat_gate = gate_prob.reshape(-1)
    own_expert = own // SPAN
    place = own % SPAN

    mine = lax.dynamic_slice_in_dim(partner, own_expert * SPAN, SPAN, axis=0)
    edge_slot = jnp.where(place == 0, own + SPAN, own - SPAN + slots_all) % slots_all
    is_edge = (place == 0) | (place == SPAN - 1)
    own_times = jnp.sum(mine == own, axis=0).astype(jnp.float32)
    edge_times = jnp.sum((mine == edge_slot) & is_edge, axis=0).astype(jnp.float32)
    scales = jnp.repeat(jnp.stack([own_times, edge_times]), hid // 2, axis=1)

    onehot = (flat_route[:, None] == jnp.arange(experts_all, dtype=jnp.int32)[None, :]).astype(
        jnp.int32
    )
    slot_rank = jnp.sum(jnp.cumsum(onehot, axis=0) * onehot, axis=1) - 1
    assigned = jnp.repeat(tokens, top_count, axis=0)
    position = flat_route * capacity + slot_rank
    rows = experts_all * capacity
    picker = (jnp.arange(rows, dtype=jnp.int32)[:, None] == position[None, :]).astype(jnp.bfloat16)
    outgoing = jnp.dot(picker, assigned, preferred_element_type=jnp.float32).astype(jnp.bfloat16)

    returned = run_experts(
        outgoing.reshape(experts_all, capacity, width),
        w_gate[0],
        w_up[0],
        w_down[0],
        scales,
        slots_all,
    ).reshape(rows, width)
    expert_out = lax.dot_general(
        picker, returned, (((0,), (0,)), ((), ())), preferred_element_type=jnp.float32
    )
    weighted = expert_out * flat_gate[:, None]
    return jnp.sum(weighted.reshape(tok_count, top_count, width), axis=1).astype(jnp.bfloat16)


def solution(mesh):
    return jax.shard_map(
        body,
        mesh=mesh,
        in_specs=(
            P(AXES, None),
            P(AXES, None),
            P(AXES, None),
            P(AXES, None, None),
            P(AXES, None, None),
            P(AXES, None, None),
            P(),
        ),
        out_specs=P(AXES, None),
        check_vma=False,
    )
```

```python
import functools

import jax
import jax.numpy as jnp
from jax import lax
from jax.experimental import pallas as pl
from jax.experimental.pallas import tpu as pltpu
from jax.sharding import PartitionSpec as P

SPAN = 4
AXES = ("grp", "loc")


MESH = pl.DeviceIdType.MESH


def expert_kernel(
    slots_all,
    n_loc,
    chunks,
    x_ref,
    wg_hbm,
    wu_hbm,
    wd_hbm,
    scale_ref,
    o_ref,
    wg,
    wu,
    wd,
    eg,
    eu,
    ed,
    rows_buf,
    up_buf,
    down_buf,
    hid_buf,
    acc_buf,
    load_sem,
    edge_send,
    edge_recv,
    ag_send,
    ag_recv,
    rs_send,
    rs_recv,
    stage_in,
    stage_out,
    disp_send,
    disp_recv,
    ret_send,
    ret_recv,
    own_sem,
    out_sem,
):
    last = SPAN - 1
    own = lax.axis_index("grp") * n_loc + lax.axis_index("loc")
    place = lax.rem(own, SPAN)
    own_e = lax.div(own, SPAN)
    experts, capacity = x_ref.shape[0], x_ref.shape[1]
    per = experts // chunks
    span_rows, width = rows_buf.shape[2], rows_buf.shape[3]
    hid = wg.shape[1]
    is_edge = (place == 0) | (place == last)

    def device(index):
        index = lax.rem(index + slots_all, slots_all)
        return (lax.div(index, n_loc), lax.rem(index, n_loc))

    barrier = pltpu.get_barrier_semaphore()

    def greet(index):
        pl.semaphore_signal(barrier, inc=1, device_id=device(index), device_id_type=MESH)

    pl.when(place < last)(lambda: greet(own + 1))
    pl.when(place > 0)(lambda: greet(own - 1))

    @pl.when(is_edge)
    def _():
        greet(own + SPAN)
        greet(own - SPAN)

    for away in range(1, experts):
        greet(own + away * SPAN)
    pl.semaphore_wait(barrier, jnp.where(is_edge, 3, 2) + experts - 1)

    def dispatch_copy(away):
        peer = lax.rem(own_e + away, experts)
        return pltpu.make_async_remote_copy(
            src_ref=x_ref.at[peer],
            dst_ref=stage_in.at[own_e],
            send_sem=disp_send.at[away],
            recv_sem=disp_recv.at[away],
            device_id=device(peer * SPAN + place),
            device_id_type=MESH,
        )

    def return_copy(peer, sender):
        return pltpu.make_async_remote_copy(
            src_ref=stage_out.at[peer],
            dst_ref=o_ref.at[sender],
            send_sem=ret_send.at[peer],
            recv_sem=ret_recv.at[sender],
            device_id=device(peer * SPAN + place),
            device_id_type=MESH,
        )

    edge_target = device(jnp.where(place == 0, own - SPAN, own + SPAN))
    edge_copies = [
        pltpu.make_async_remote_copy(
            src_ref=src,
            dst_ref=dst,
            send_sem=edge_send.at[k],
            recv_sem=edge_recv.at[k],
            device_id=edge_target,
            device_id_type=MESH,
        )
        for k, (src, dst) in enumerate(((wg_hbm, eg), (wu_hbm, eu), (wd_hbm, ed)))
    ]
    loads = [
        pltpu.make_async_copy(src, dst, load_sem.at[k])
        for k, (src, dst) in enumerate(((wg_hbm, wg), (wu_hbm, wu), (wd_hbm, wd)))
    ]

    def mirrored(way, value):
        return value if way == 0 else last - value

    def gather_copy(way, c, step):
        mine = mirrored(way, place)
        source = mirrored(way, jnp.clip(mine - (step - 1), 0, last))
        return pltpu.make_async_remote_copy(
            src_ref=rows_buf.at[c, source],
            dst_ref=rows_buf.at[c, source],
            send_sem=ag_send.at[way, c, step - 1],
            recv_sem=ag_recv.at[way, c, step - 1],
            device_id=device(own + 1 if way == 0 else own - 1),
            device_id_type=MESH,
        )

    def gather_sends(way, step):
        mine = mirrored(way, place)
        return (mine < last) & (mine >= step - 1)

    def gather_gets(way, step):
        return mirrored(way, place) >= step

    def gather_start(c, step):
        for way in range(2):
            pl.when(gather_sends(way, step))(lambda way=way: gather_copy(way, c, step).start())

    def gather_wait(c, step):
        for way in range(2):
            pl.when(gather_gets(way, step))(lambda way=way: gather_copy(way, c, step).wait_recv())

    def gather_drain(c):
        for step in range(1, SPAN):
            for way in range(2):
                pl.when(gather_sends(way, step))(
                    lambda way=way, step=step: gather_copy(way, c, step).wait_send()
                )

    side = (up_buf, down_buf)

    def reduce_target(way, step):
        mine = mirrored(way, place)
        return mirrored(way, jnp.clip(SPAN + mine - step, 0, last))

    def reduce_copy(way, c, step, first):
        target = reduce_target(way, step)
        return pltpu.make_async_remote_copy(
            src_ref=rows_buf.at[c, target] if first else side[way].at[c, target],
            dst_ref=side[way].at[c, target],
            send_sem=rs_send.at[way, c, step - 1],
            recv_sem=rs_recv.at[way, c, step - 1],
            device_id=device(own + 1 if way == 0 else own - 1),
            device_id_type=MESH,
        )

    def reduce_sends(way, step):
        mine = mirrored(way, place)
        return (mine <= step - 1) & (mine < last) & (mine > 0)

    def reduce_gets(way, step):
        mine = mirrored(way, place)
        return (mine >= 1) & (mine <= step)

    cols = 512 if width % 512 == 0 else 128

    def reduce_start(c, step):
        for way in range(2):
            pl.when(mirrored(way, place) == 0)(
                lambda way=way: reduce_copy(way, c, step, True).start()
            )

            @pl.when(reduce_sends(way, step))
            def _(way=way):
                target = reduce_target(way, step)

                @pl.loop(0, width // cols)
                def _(k):
                    at = pl.ds(pl.multiple_of(k * cols, cols), cols)
                    side[way][c, target, :, at] = (
                        side[way][c, target, :, at].astype(jnp.float32)
                        + rows_buf[c, target, :, at].astype(jnp.float32)
                    ).astype(jnp.bfloat16)

                reduce_copy(way, c, step, False).start()

    def reduce_wait(c, step):
        for way in range(2):
            pl.when(reduce_gets(way, step))(
                lambda way=way: reduce_copy(way, c, step, False).wait_recv()
            )

    def reduce_drain(c):
        for step in range(1, SPAN):
            for way in range(2):
                mine = mirrored(way, place)
                pl.when((mine <= step - 1) & (mine < last))(
                    lambda way=way, step=step: reduce_copy(way, c, step, False).wait_send()
                )

    kept = pltpu.make_async_copy(stage_out.at[own_e], o_ref.at[own_e], out_sem)

    def unpack():
        @pl.loop(0, width // cols)
        def _(k):
            at = pl.ds(pl.multiple_of(k * cols, cols), cols)
            for j in range(experts):
                acc_buf[pl.ds(j * capacity, capacity), :] = stage_in[j, :, at].astype(jnp.float32)
            for c in range(chunks):
                rows_buf[c, place, :, at] = acc_buf[
                    pl.ds(c * span_rows, span_rows), :
                ].astype(jnp.bfloat16)

    def reduce_finish(c):
        first = pl.ds(0, span_rows)

        @pl.loop(0, width // cols)
        def _(k):
            at = pl.ds(pl.multiple_of(k * cols, cols), cols)
            acc_buf[first, :] = rows_buf[c, place, :, at].astype(jnp.float32)
            for way in range(2):

                @pl.when(mirrored(way, place) > 0)
                def _(way=way):
                    acc_buf[first, :] += side[way][c, place, :, at].astype(jnp.float32)

            for j in range(per):
                stage_out[c * per + j, :, at] = acc_buf[
                    pl.ds(j * capacity, capacity), :
                ].astype(jnp.bfloat16)

        for j in range(per):
            peer = c * per + j
            pl.when(own_e != peer)(lambda peer=peer: return_copy(peer, own_e).start())
            pl.when(own_e == peer)(lambda: kept.start())

    total_rows = SPAN * span_rows
    depth = 512 if width % 512 == 0 else 128

    def make_hidden(c, gate_w, up_w, which):
        def step(k, carry):
            gate_part, up_part = carry
            at = pl.ds(pl.multiple_of(k * depth, depth), depth)
            block = rows_buf[c, :, :, at].reshape(total_rows, depth)
            gate_part += jnp.dot(block, gate_w[at, :], preferred_element_type=jnp.float32)
            up_part += jnp.dot(block, up_w[at, :], preferred_element_type=jnp.float32)
            return gate_part, up_part

        zero = jnp.zeros((total_rows, hid), jnp.float32)
        gate_part, up_part = lax.fori_loop(0, width // depth, step, (zero, zero))
        value = gate_part / (1.0 + jnp.exp(-gate_part)) * up_part
        hid_buf[which] = (value * scale_ref[which : which + 1, :]).astype(jnp.bfloat16)

    def make_partial(c, both):
        @pl.loop(0, width // cols)
        def _(k):
            at = pl.ds(pl.multiple_of(k * cols, cols), cols)
            out = jnp.dot(hid_buf[0], wd[:, at], preferred_element_type=jnp.float32)
            if both:
                out += jnp.dot(hid_buf[1], ed[:, at], preferred_element_type=jnp.float32)
            rows_buf[c, :, :, at] = out.astype(jnp.bfloat16).reshape(SPAN, span_rows, cols)

    def compute(c):
        if c == 0:
            for copy in loads:
                copy.wait()
        make_hidden(c, wg, wu, 0)

        @pl.when(is_edge)
        def _():
            if c == 0:
                for copy in edge_copies[:2]:
                    copy.wait_recv()
            make_hidden(c, eg, eu, 1)
            if c == 0:
                edge_copies[2].wait_recv()

        gather_drain(c)
        pl.when(is_edge)(lambda: make_partial(c, True))
        pl.when(jnp.logical_not(is_edge))(lambda: make_partial(c, False))

    own_copy = pltpu.make_async_copy(x_ref.at[own_e], stage_in.at[own_e], own_sem)
    own_copy.start()
    for away in range(1, experts):
        dispatch_copy(away).start()

    @pl.when(is_edge)
    def _():
        for copy in edge_copies:
            copy.start()

    for copy in loads:
        copy.start()
    own_copy.wait()
    for away in range(1, experts):
        dispatch_copy(away).wait_recv()
    unpack()
    gather_start(0, 1)
    for step in range(1, SPAN):
        if step > 1:
            gather_start(0, step)
        gather_wait(0, step)
    if chunks > 1:
        gather_start(1, 1)
    compute(0)
    for c in range(chunks):
        more = c + 1 < chunks
        reduce_start(c, 1)
        if c > 0:
            reduce_finish(c - 1)
        for step in range(1, SPAN - 1):
            if more:
                gather_wait(c + 1, step)
                gather_start(c + 1, step + 1)
            reduce_wait(c, step)
            reduce_start(c, step + 1)
        if more:
            gather_wait(c + 1, SPAN - 1)
            if c + 2 < chunks:
                gather_start(c + 2, 1)
            compute(c + 1)
        reduce_wait(c, SPAN - 1)
    reduce_finish(chunks - 1)
    for c in range(chunks):
        reduce_drain(c)
    for away in range(1, experts):
        dispatch_copy(away).wait_send()
    for peer in range(experts):

        @pl.when(own_e != peer)
        def _(peer=peer):
            return_copy(peer, peer).wait_send()
            return_copy(peer, peer).wait_recv()

    kept.wait()

    @pl.when(is_edge)
    def _():
        for copy in edge_copies:
            copy.wait_send()


def run_experts(received, w_gate, w_up, w_down, scales, slots_all):
    experts, capacity, width = received.shape
    rows = experts * capacity
    hid = w_gate.shape[1]
    chunks = 2 if rows % 32 == 0 and experts % 2 == 0 else 1
    span_rows = rows // chunks
    anywhere = pl.BlockSpec(memory_space=pl.ANY)
    dma = pltpu.SemaphoreType.DMA
    bf16 = jnp.bfloat16
    out = pl.pallas_call(
        functools.partial(expert_kernel, slots_all, lax.axis_size("loc"), chunks),
        out_shape=jax.ShapeDtypeStruct((experts, capacity, width), bf16),
        in_specs=[anywhere] * 4 + [pl.BlockSpec(memory_space=pltpu.VMEM)],
        out_specs=anywhere,
        scratch_shapes=[
            pltpu.VMEM((width, hid), bf16),
            pltpu.VMEM((width, hid), bf16),
            pltpu.VMEM((hid, width), bf16),
            pltpu.VMEM((width, hid), bf16),
            pltpu.VMEM((width, hid), bf16),
            pltpu.VMEM((hid, width), bf16),
            pltpu.VMEM((chunks, SPAN, span_rows, width), bf16),
            pltpu.VMEM((chunks, SPAN, span_rows, width), bf16),
            pltpu.VMEM((chunks, SPAN, span_rows, width), bf16),
            pltpu.VMEM((2, SPAN * span_rows, hid), bf16),
            pltpu.VMEM((rows, 512 if width % 512 == 0 else 128), jnp.float32),
            dma((3,)),
            dma((3,)),
            dma((3,)),
            dma((2, chunks, SPAN - 1)),
            dma((2, chunks, SPAN - 1)),
            dma((2, chunks, SPAN - 1)),
            dma((2, chunks, SPAN - 1)),
            pltpu.VMEM((experts, capacity, width), bf16),
            pltpu.VMEM((experts, capacity, width), bf16),
            dma((experts,)),
            dma((experts,)),
            dma((experts,)),
            dma((experts,)),
            dma,
            dma,
        ],
        compiler_params=pltpu.CompilerParams(
            collective_id=0, has_side_effects=True, vmem_limit_bytes=62 * 1024 * 1024
        ),
        name="experts",
    )(received, w_gate, w_up, w_down, scales)
    return out


def body(tokens, route, gate_prob, w_gate, w_up, w_down, partner):
    slots_all = lax.axis_size(AXES)
    own = lax.axis_index(AXES)
    tok_count, top_count = route.shape
    width = tokens.shape[1]
    hid = w_gate.shape[2]
    capacity = max(2, tok_count * top_count * SPAN * 5 // (4 * slots_all))
    experts_all = slots_all // SPAN
    flat_route = route.reshape(-1)
    flat_gate = gate_prob.reshape(-1)
    own_expert = own // SPAN
    place = own % SPAN

    mine = lax.dynamic_slice_in_dim(partner, own_expert * SPAN, SPAN, axis=0)
    edge_slot = jnp.where(place == 0, own + SPAN, own - SPAN + slots_all) % slots_all
    is_edge = (place == 0) | (place == SPAN - 1)
    own_times = jnp.sum(mine == own, axis=0).astype(jnp.float32)
    edge_times = jnp.sum((mine == edge_slot) & is_edge, axis=0).astype(jnp.float32)
    scales = jnp.repeat(jnp.stack([own_times, edge_times]), hid // 2, axis=1)

    onehot = (flat_route[:, None] == jnp.arange(experts_all, dtype=jnp.int32)[None, :]).astype(
        jnp.int32
    )
    slot_rank = jnp.sum(jnp.cumsum(onehot, axis=0) * onehot, axis=1) - 1
    assigned = jnp.repeat(tokens, top_count, axis=0)
    position = flat_route * capacity + slot_rank
    rows = experts_all * capacity
    places = jnp.arange(rows, dtype=jnp.int32).reshape(experts_all, capacity)
    picker = (places[:, :, None] == position[None, None, :]).astype(jnp.bfloat16)
    spread = jnp.broadcast_to(assigned[None], (experts_all,) + assigned.shape)
    outgoing = lax.dot_general(
        picker, spread, (((2,), (1,)), ((0,), (0,))), preferred_element_type=jnp.float32
    ).astype(jnp.bfloat16)
    returned = run_experts(
        outgoing,
        w_gate[0],
        w_up[0],
        w_down[0],
        scales,
        slots_all,
    )
    expert_out = lax.dot_general(
        picker, returned, (((0, 1), (0, 1)), ((), ())), preferred_element_type=jnp.float32
    )
    weighted = expert_out * flat_gate[:, None]
    return jnp.sum(weighted.reshape(tok_count, top_count, width), axis=1).astype(jnp.bfloat16)


def solution(mesh):
    return jax.shard_map(
        body,
        mesh=mesh,
        in_specs=(
            P(AXES, None),
            P(AXES, None),
            P(AXES, None),
            P(AXES, None, None),
            P(AXES, None, None),
            P(AXES, None, None),
            P(),
        ),
        out_specs=P(AXES, None),
        check_vma=False,
    )
```
